32 devices in a mesh: pairs: 8 (over z, x), hours: 4 (over y, core).
Axes of the slice: x: 2, y: 2, z: 4, core: 2. Of those that a mesh axis runs over, the one named last changes fastest.
Arguments:
- records: bfloat16 [1024, 4, 3600], P('pairs', 'hours'), may hold values from -100 to 100
- usable: int32 [1024, 4], P('pairs', 'hours'), may hold values from 0 to 1, as said below
- pair_blocks: int32 [8, 2], P('pairs'), may hold values from 0 to 7
Outputs:
- correlations: float32 [8, 128, 128, 256], P('pairs', 'hours')
The draws below stay inside these ranges and needn't reach their ends.
Inputs may be any that keep to these rules, and one draw needn't show every extreme that they name: Some stations are usable in no hour at all. `pair_blocks`: each row names two station blocks; a block may appear in many rows and both entries may be equal.
All inputs are finite; a program needn't handle non-finite values.
Results may differ from the reference program's by a relative error of at most 0.0071.
Values may be sent and summed in bfloat16 or wider, within the bound.
A program may use at most 128 MiB of HBM per device.

```python
import math
import jax
import jax.numpy as jnp
import numpy as np
from jax import lax

SB = 128
L = 3600
F = 512
W = 32
F0 = 64
LAGS = 256
STATIONS = 1024
HOURS = 4
PAIRS_ALL = 8


def draw_records(key, part):
    key_scale, key_base = jax.random.split(key, 2)
    station_scale = jnp.exp(jax.random.uniform(key_scale, (STATIONS, 1, 1), jnp.float32, 0.0, math.log(10.0)))
    base = jax.random.normal(key_base, (STATIONS, HOURS, L), jnp.float32)
    return (station_scale * base).astype(jnp.bfloat16)


def draw_usable(key, part):
    key_draws, key_dead = jax.random.split(key, 2)
    hour_rank = jnp.arange(HOURS, dtype=jnp.int32)
    threshold = 30 + 65 * hour_rank // max(HOURS - 1, 1)
    rolls = jax.random.randint(key_draws, (STATIONS, HOURS), 0, 100)
    alive = jax.random.randint(key_dead, (STATIONS, 1), 0, 16) != 0
    return jnp.where((rolls < threshold[None, :]) & alive, 1, 0).astype(jnp.int32)


def with_ends(entries, rng, low, top_value):
    shape = entries.shape
    spot = [jax.random.randint(jax.random.fold_in(rng, axis), (), 0, shape[axis]) for axis in range(len(shape))]
    entries = entries.at[tuple(spot)].set(low)
    longest = shape.index(max(shape))
    spot[longest] = (spot[longest] + 1) % shape[longest]
    return entries.at[tuple(spot)].set(top_value)


def rank_table(count, skew):
    loads = [(1 << 20) // math.isqrt(standing ** skew) + 1 for standing in range(1, count + 1)]
    width = 1 + sum(loads) // (1 << 30)
    return np.cumsum(np.array([max(1, weight // width) for weight in loads]))


def skewed_ids(stream_key, dims, count, skew):
    listing = rank_table(count, skew)
    pick = jax.random.randint(jax.random.fold_in(stream_key, 1), dims, 0, int(listing[count - 1]))
    rank = jnp.searchsorted(jnp.asarray(listing, jnp.int32), pick, side="right")
    return jax.random.permutation(jax.random.fold_in(stream_key, 2), count)[rank].astype(jnp.int32)


def setup_inputs(seed: int = 0) -> dict:
    key_of = jax.random.split(jax.random.key(seed), 4)
    return {
        "records": draw_records(jax.random.fold_in(key_of[3], 71), 0),
        "usable": draw_usable(jax.random.fold_in(key_of[3], 71), 0),
        "pair_blocks": with_ends(skewed_ids(key_of[2], (PAIRS_ALL, 2), STATIONS // SB, 2), jax.random.fold_in(key_of[2], 3), 0, (STATIONS // SB) - 1).astype(jnp.int32),
    }


def spectrum_table():
    extent = F + 2 * W
    freq_bins = F0 - W + jnp.arange(extent, dtype=jnp.int32)
    samples = jnp.arange(L, dtype=jnp.int32)
    phases = samples[:, None] * freq_bins[None, :] % L
    angles = 2.0 * math.pi / L * phases.astype(jnp.float32)
    factor = 1.0 / math.sqrt(L)
    return jnp.concatenate([jnp.cos(angles) * factor, -jnp.sin(angles) * factor], axis=1).astype(jnp.bfloat16)

def smoothing_matrix():
    extent = F + 2 * W
    source = jnp.arange(extent, dtype=jnp.int32)[:, None]
    target = jnp.arange(F, dtype=jnp.int32)[None, :]
    spacing = source - target
    within = (spacing >= 0) & (spacing <= 2 * W)
    return jnp.where(within, jnp.float32(1.0 / (2 * W + 1)), jnp.float32(0.0)).astype(jnp.float32)

def lag_weights():
    freq_bins = F0 + jnp.arange(F, dtype=jnp.int32)
    shifts = jnp.arange(LAGS, dtype=jnp.int32) - LAGS // 2
    phases = freq_bins[:, None] * shifts[None, :] % L
    angles = 2.0 * math.pi / L * phases.astype(jnp.float32)
    factor = 1.0 / math.sqrt(F)
    return jnp.concatenate([jnp.cos(angles) * factor, -jnp.sin(angles) * factor], axis=0).astype(jnp.bfloat16)

def whiten(signal, usable_flags):
    station_rows, hour_count = (signal.shape[0], signal.shape[1])
    flat = signal.reshape(station_rows * hour_count, L).astype(jnp.float32)
    spectra = jnp.dot(flat, spectrum_table().astype(jnp.float32), precision=lax.Precision.HIGHEST)
    extent = F + 2 * W
    real_part = spectra[:, :extent]
    imag_part = spectra[:, extent:]
    power = real_part * real_part + imag_part * imag_part
    smooth = jnp.dot(power, smoothing_matrix(), precision=lax.Precision.HIGHEST)
    weight = usable_flags.reshape(station_rows * hour_count, 1).astype(jnp.float32) / jnp.sqrt(smooth + 1e-05)
    whitened = jnp.concatenate([real_part[:, W:W + F] * weight, imag_part[:, W:W + F] * weight], axis=1)
    return whitened.astype(jnp.bfloat16).reshape(station_rows, hour_count, 2 * F)

def hour_cross(first_hour, second_hour):
    first_real = first_hour[:, :F].astype(jnp.float32)
    first_imag = first_hour[:, F:].astype(jnp.float32)
    second_real = second_hour[:, :F].astype(jnp.float32)
    second_imag = second_hour[:, F:].astype(jnp.float32)
    cross_real = first_real[:, None, :] * second_real[None, :, :] + first_imag[:, None, :] * second_imag[None, :, :]
    cross_imag = first_imag[:, None, :] * second_real[None, :, :] - first_real[:, None, :] * second_imag[None, :, :]
    return jnp.concatenate([cross_real, cross_imag], axis=2).astype(jnp.bfloat16)

def correlate(first_block, second_block, first_flags, second_flags, weights):
    first_rows = first_block.shape[0]
    second_rows = second_block.shape[0]
    weights_wide = weights.astype(jnp.float32)

    def add_hour(hour_step, running):
        first_hour = lax.dynamic_index_in_dim(first_block, hour_step, 1, keepdims=False)
        second_hour = lax.dynamic_index_in_dim(second_block, hour_step, 1, keepdims=False)
        cross = hour_cross(first_hour, second_hour).astype(jnp.float32)
        lagged = jnp.dot(cross.reshape(first_rows * second_rows, 2 * F), weights_wide, precision=lax.Precision.HIGHEST)
        return running + lagged.reshape(first_rows, second_rows, LAGS)
    stacks = lax.fori_loop(0, first_block.shape[1], add_hour, jnp.zeros((first_rows, second_rows, LAGS), jnp.float32))
    counts = jnp.dot(first_flags.astype(jnp.float32), second_flags.astype(jnp.float32).T, precision=lax.Precision.HIGHEST)
    return (stacks, counts)

def reference(records, usable, pair_blocks):
    whitened = whiten(records, usable)
    weights = lag_weights()

    def one_tile(blocks_pair):
        first_start = (blocks_pair[0] * SB).astype(jnp.int32)
        second_start = (blocks_pair[1] * SB).astype(jnp.int32)
        first_block = lax.dynamic_slice_in_dim(whitened, first_start, SB, 0)
        second_block = lax.dynamic_slice_in_dim(whitened, second_start, SB, 0)
        first_flags = lax.dynamic_slice_in_dim(usable, first_start, SB, 0)
        second_flags = lax.dynamic_slice_in_dim(usable, second_start, SB, 0)
        stacks, counts = correlate(first_block, second_block, first_flags, second_flags, weights)
        return stacks / jnp.maximum(counts, 1.0)[:, :, None]
    return lax.map(one_tile, pair_blocks)
```

```python
import functools
import math

import jax
import jax.numpy as jnp
import numpy as np
from jax import lax
from jax.experimental import pallas as pl
from jax.experimental.pallas import tpu as pltpu
from jax.sharding import PartitionSpec as P

L = 3600
F = 512
W = 32
F0 = 64
LAGS = 256
EXTENT = F + 2 * W
HALF = L // 2
HE = EXTENT // 2
HF = F // 2
CORES = 2
MESH = pl.DeviceIdType.MESH


def cos_sin(phases, length, scale):
    angles = np.float32(2.0 * math.pi / length) * (phases % length).astype(np.float32)
    wide = angles.astype(np.float64)
    scale = np.float32(scale)
    return np.cos(wide).astype(np.float32) * scale, -np.sin(wide).astype(np.float32) * scale


def spectrum_tables():
    bins = F0 - W + np.arange(EXTENT)
    c, q = cos_sin(np.arange(HALF)[:, None] * bins[None, :], L, 1.0 / math.sqrt(L))
    even = np.concatenate([c[:, 0::2], q[:, 0::2]], axis=1)
    odd = np.concatenate([c[:, 1::2], q[:, 1::2]], axis=1)
    return even.astype(jnp.bfloat16), odd.astype(jnp.bfloat16)


def window_ones():
    source = np.concatenate([np.arange(0, EXTENT, 2), np.arange(1, EXTENT, 2)])
    target = np.concatenate([np.arange(0, F, 2), np.arange(1, F, 2)])
    gap = source[:, None] - target[None, :]
    return ((gap >= 0) & (gap <= 2 * W)).astype(np.float32).astype(jnp.bfloat16)


def lag_weights():
    order = np.concatenate([np.arange(0, F, 2), np.arange(1, F, 2)])
    shifts = np.arange(LAGS) - LAGS // 2
    c, s = cos_sin((F0 + order)[:, None] * shifts[None, :], L, 1.0 / math.sqrt(F))
    return np.concatenate([c, s], axis=0).astype(jnp.bfloat16)


def split_hi_lo(value):
    high = value.astype(jnp.bfloat16)
    low = (value - high.astype(jnp.float32)).astype(jnp.bfloat16)
    return jnp.concatenate([high, low], axis=0)


def whiten_kernel(u_ref, v_ref, flag_ref, even_ref, odd_ref, ones_ref, out_ref):
    rows = out_ref.shape[0]

    def transform(x_ref, table_ref):
        both = jnp.dot(x_ref[...], table_ref[...], preferred_element_type=jnp.float32)
        both = both[:rows] + both[rows:]
        return both[:, :HE], both[:, HE:]

    re_even, im_even = transform(u_ref, even_ref)
    re_odd, im_odd = transform(v_ref, odd_ref)
    power = jnp.concatenate(
        [re_even * re_even + im_even * im_even, re_odd * re_odd + im_odd * im_odd], axis=1
    )
    total = jnp.dot(split_hi_lo(power), ones_ref[...], preferred_element_type=jnp.float32)
    smooth = (total[:rows] + total[rows:]) * jnp.float32(1.0 / (2 * W + 1))
    weight = flag_ref[...] / jnp.sqrt(smooth + 1e-05)
    w2 = W // 2
    out_ref[:, 0:HF] = (re_even[:, w2 : w2 + HF] * weight[:, :HF]).astype(jnp.bfloat16)
    out_ref[:, HF:F] = (re_odd[:, w2 : w2 + HF] * weight[:, HF:]).astype(jnp.bfloat16)
    out_ref[:, F : F + HF] = (im_even[:, w2 : w2 + HF] * weight[:, :HF]).astype(jnp.bfloat16)
    out_ref[:, F + HF :] = (im_odd[:, w2 : w2 + HF] * weight[:, HF:]).astype(jnp.bfloat16)


def exchange_kernel(
    pairs, width, hours, pair_ref, w_ref, f_ref, bj, bi, bf,
    *scratch,
):
    g = scratch[:hours]
    (
        gf, sj, si, sf, zx_send, zx_recv, j_send, j_recv, relay_send, i_send, i_recv,
        f_send, f_recv, local_sem, keep_sem,
    ) = scratch[hours:]
    depth = pairs // width
    rows = w_ref.shape[0]
    part = rows // hours
    p = lax.axis_index("pairs")
    me = lax.axis_index("hours")
    z, x = p // width, p % width
    y, core = me // CORES, me % CORES
    partner = y * CORES + (1 - core)
    flags_unit = hours

    steps = (
        (z + 1 < depth, p + width),
        (z > 0, p - width),
        (x + 1 < width, p + 1),
        (x > 0, p - 1),
    )

    barrier = pltpu.get_barrier_semaphore()
    for exists, target in steps:
        @pl.when(exists)
        def _(target=target):
            pl.semaphore_signal(barrier, inc=1, device_id={"pairs": target}, device_id_type=MESH)
    for k in range(1, hours):
        pl.semaphore_signal(
            barrier, inc=1, device_id={"hours": (me + k) % hours}, device_id_type=MESH
        )
    near = sum(e.astype(jnp.int32) for e, _ in steps)
    pl.semaphore_wait(barrier, near + hours - 1)

    pending = []

    def slot(b, u):
        return gf.at[b] if u == flags_unit else g[u].at[b]

    def own(u):
        return f_ref if u == flags_unit else w_ref.at[pl.ds(u * part, part)]

    def forward(cond, b, u, way, is_own=False):
        exists, target = steps[way]
        both = exists if cond is None else jnp.logical_and(cond, exists)

        def make():
            return pltpu.make_async_remote_copy(
                src_ref=own(u) if is_own else slot(b, u),
                dst_ref=slot(b, u),
                send_sem=zx_send.at[way, b, u],
                recv_sem=zx_recv.at[b, u],
                device_id={"pairs": target},
                device_id_type=MESH,
            )

        @pl.when(both)
        def _():
            make().start()
        pending.append((both, make))

    def arrived(b, u):
        pltpu.make_async_remote_copy(
            src_ref=slot(b, u), dst_ref=slot(b, u), send_sem=zx_send.at[0, b, u],
            recv_sem=zx_recv.at[b, u], device_id={"pairs": p}, device_id_type=MESH,
        ).wait_recv()

    def send_own(u):
        for way in range(4):
            forward(None, p, u, way, is_own=True)

    keep = [
        pltpu.make_async_copy(own(u), slot(p, u), keep_sem.at[u]) for u in range(hours + 1)
    ]
    for copy in keep:
        copy.start()

    def gather(u):
        for d in range(1, depth):
            for way, b, cond in (
                (0, p - d * width, z - d >= 0),
                (1, p + d * width, z + d < depth),
            ):
                @pl.when(cond)
                def _(b=b):
                    arrived(b, u)
                for out in (way, 2, 3):
                    forward(cond, b, u, out)
        for d in range(1, width):
            for zz in range(depth):
                for way, b, cond in (
                    (2, zz * width + x - d, x - d >= 0),
                    (3, zz * width + x + d, x + d < width),
                ):
                    @pl.when(cond)
                    def _(b=b):
                        arrived(b, u)
                    if width > 2:
                        forward(cond, b, u, way)

    late = []

    def remote(src, dst, send_sem, recv_sem, target):
        copy = pltpu.make_async_remote_copy(
            src_ref=src, dst_ref=dst, send_sem=send_sem, recv_sem=recv_sem,
            device_id={"hours": target}, device_id_type=MESH,
        )
        copy.start()
        late.append(copy)

    def share(u):
        span = pl.ds(u * part, part)
        keep[u].wait()
        sj[u] = g[u][pair_ref[0, 1]]
        si[u] = g[u][pair_ref[0, 0]]
        for k in range(1, hours // CORES):
            target = ((y + k) % (hours // CORES)) * CORES + core
            remote(sj.at[u], bj.at[me, span], j_send.at[k, u], j_recv.at[me, u], target)
        remote(sj.at[u], bj.at[me, span], j_send.at[0, u], j_recv.at[me, u], partner)
        to_other = me != u

        def make():
            return pltpu.make_async_remote_copy(
                src_ref=si.at[u], dst_ref=bi.at[me], send_sem=i_send.at[u],
                recv_sem=i_recv.at[me], device_id={"hours": u}, device_id_type=MESH,
            )

        @pl.when(to_other)
        def _():
            make().start()
        pending.append((to_other, make))

        @pl.when(me == u)
        def _():
            pltpu.make_async_copy(si.at[u], bi.at[me], local_sem.at[2]).start()
        pltpu.make_async_copy(sj.at[u], bj.at[me, span], local_sem.at[3 + u]).start()

    def got(sem, ref):
        pltpu.make_async_remote_copy(
            src_ref=ref, dst_ref=ref, send_sem=sem, recv_sem=sem,
            device_id={"hours": me}, device_id_type=MESH,
        ).wait_recv()

    def relay(u):
        span = pl.ds(u * part, part)
        for k in range(1, hours // CORES):
            peer = ((y + k) % (hours // CORES)) * CORES + core
            got(j_recv.at[peer, u], bj.at[peer, span])
            remote(
                bj.at[peer, span], bj.at[peer, span], relay_send.at[k, u],
                j_recv.at[peer, u], partner,
            )

    send_own(flags_unit)
    send_own(0)
    for u in range(hours):
        if u + 1 < hours:
            send_own(u + 1)
        if u == 0:
            gather(flags_unit)
        gather(u)
        if u == 0:
            keep[flags_unit].wait()
            sf[0] = gf[pair_ref[0, 0]]
            sf[1] = gf[pair_ref[0, 1]]
            for k in range(1, hours):
                target = (me + k) % hours
                remote(sf, bf.at[me], f_send.at[k], f_recv.at[me], target)
            pltpu.make_async_copy(sf, bf.at[me], local_sem.at[3 + hours]).start()
        share(u)
        if u > 0:
            relay(u - 1)
    relay(hours - 1)

    for u in range(hours):
        span = pl.ds(u * part, part)
        for k in range(hours // CORES):
            peer = ((y + k) % (hours // CORES)) * CORES + (1 - core)
            got(j_recv.at[peer, u], bj.at[peer, span])
        pltpu.make_async_copy(sj.at[u], bj.at[me, span], local_sem.at[3 + u]).wait()
    for k in range(1, hours):
        peer = (me + k) % hours
        got(i_recv.at[peer], bi.at[peer])
        got(f_recv.at[peer], bf.at[peer])
    pltpu.make_async_copy(sf, bf.at[me], local_sem.at[3 + hours]).wait()
    pltpu.make_async_copy(si.at[0], bi.at[me], local_sem.at[2]).wait()
    for cond, make in pending:
        @pl.when(cond)
        def _(make=make):
            make().wait_send()
    for copy in late:
        copy.wait_send()


def exchange(pair_blocks, whitened, marks, pairs, width, hours):
    rows, cols = whitened.shape
    part = rows // hours
    any_space = pl.BlockSpec(memory_space=pl.ANY)
    dma = pltpu.SemaphoreType.DMA
    groups = hours // CORES
    return pl.pallas_call(
        functools.partial(exchange_kernel, pairs, width, hours),
        out_shape=(
            jax.ShapeDtypeStruct((hours, rows, cols), jnp.bfloat16),
            jax.ShapeDtypeStruct((hours, part, cols), jnp.bfloat16),
            jax.ShapeDtypeStruct((hours, 2) + marks.shape, jnp.bfloat16),
        ),
        in_specs=[pl.BlockSpec(memory_space=pltpu.SMEM), any_space, any_space],
        out_specs=(any_space, any_space, any_space),
        scratch_shapes=[pltpu.VMEM((pairs, part, cols), jnp.bfloat16)] * hours + [
            pltpu.VMEM((pairs,) + marks.shape, jnp.bfloat16),
            pltpu.VMEM((hours, part, cols), jnp.bfloat16),
            pltpu.VMEM((hours, part, cols), jnp.bfloat16),
            pltpu.VMEM((2,) + marks.shape, jnp.bfloat16),
            dma((4, pairs, hours + 1)),
            dma((pairs, hours + 1)),
            dma((groups, hours)),
            dma((hours, hours)),
            dma((groups, hours)),
            dma((hours,)),
            dma((hours,)),
            dma((hours,)),
            dma((hours,)),
            dma((hours + 4,)),
            dma((hours + 1,)),
        ],
        compiler_params=pltpu.CompilerParams(
            collective_id=0, has_side_effects=True, vmem_limit_bytes=32 << 20
        ),
        name="exchange",
    )(pair_blocks, whitened, marks)


GROUP = 8


def stack_kernel(hours, work, me_ref, bi_ref, bj_ref, bf_ref, g_ref, out_ref, af, cross, recip):
    step = pl.program_id(0)
    rows = bj_ref.shape[1]
    first_rows = bi_ref.shape[1]

    @pl.when(step == 0)
    def _():
        af[...] = bi_ref[...].astype(jnp.float32)
        first = bf_ref[:, 0, 0, :]
        second = bf_ref[:, 1, 0, :]
        counts = lax.dot_general(
            second, first, (((0,), (0,)), ((), ())), preferred_element_type=jnp.float32
        )
        recip[...] = 1.0 / jnp.maximum(counts, 1.0)

    block = 64
    for a in range(GROUP):
        row = pl.ds(pl.multiple_of(step * GROUP, GROUP), GROUP)
        for c in range(F // 128):
            lo, hi = c * 128, F + c * 128
            heads = []
            for h in range(hours):
                ar = af[h, row, lo : lo + 128][a : a + 1]
                ai = af[h, row, hi : hi + 128][a : a + 1]
                heads.append(
                    tuple(jnp.broadcast_to(t, (block, 128)).astype(work) for t in (ar, ai))
                )
            for r in range(0, rows, block):
                real = imag = None
                for h in range(hours):
                    ar, ai = heads[h]
                    br = bj_ref[h, r : r + block, lo : lo + 128].astype(work)
                    bm = bj_ref[h, r : r + block, hi : hi + 128].astype(work)
                    re = ar * br + ai * bm
                    im = ai * br - ar * bm
                    real = re if real is None else real + re
                    imag = im if imag is None else imag + im
                at = a * rows + r
                cross[at : at + block, lo : lo + 128] = real.astype(jnp.bfloat16)
                cross[at : at + block, hi : hi + 128] = imag.astype(jnp.bfloat16)
    lagged = jnp.dot(cross[...], g_ref[...], preferred_element_type=jnp.float32)
    offset = me_ref[0] * first_rows + step * GROUP
    scale = pltpu.roll(recip[...], (rows - offset) % rows, 1)
    for a in range(GROUP):
        out_ref[0, a] = lagged[a * rows : (a + 1) * rows] * scale[:, a : a + 1]


def stack(me, bi, bj, bf, weights, work):
    hours, first_rows, cols = bi.shape
    rows = bj.shape[1]
    full = lambda a: pl.BlockSpec(a.shape, lambda i, *_: (0,) * a.ndim, pipeline_mode=pl.Buffered(1))
    return pl.pallas_call(
        functools.partial(stack_kernel, hours, work),
        grid_spec=pltpu.PrefetchScalarGridSpec(
            num_scalar_prefetch=1,
            grid=(first_rows // GROUP,),
            in_specs=[full(bi), full(bj), full(bf), full(weights)],
            out_specs=pl.BlockSpec((1, GROUP, rows, LAGS), lambda i, *_: (0, i, 0, 0)),
            scratch_shapes=[
                pltpu.VMEM((hours, first_rows, cols), jnp.float32),
                pltpu.VMEM((GROUP * rows, cols), jnp.bfloat16),
                pltpu.VMEM((rows, rows), jnp.float32),
            ],
        ),
        out_shape=jax.ShapeDtypeStruct((1, first_rows, rows, LAGS), jnp.float32),
        compiler_params=pltpu.CompilerParams(vmem_limit_bytes=48 << 20),
        name="stack",
    )(me, bi, bj, bf, weights)


def whiten(records, usable):
    rows = records.shape[0]
    flat = records.reshape(rows, L).astype(jnp.float32)
    u = split_hi_lo(flat[:, :HALF] + flat[:, HALF:])
    v = split_hi_lo(flat[:, :HALF] - flat[:, HALF:])
    even, odd = spectrum_tables()
    flags = usable.astype(jnp.float32).reshape(rows, 1)
    return pl.pallas_call(
        whiten_kernel,
        out_shape=jax.ShapeDtypeStruct((rows, 2 * F), jnp.bfloat16),
        in_specs=[pl.BlockSpec(memory_space=pltpu.VMEM)] * 6,
        out_specs=pl.BlockSpec(memory_space=pltpu.VMEM),
        compiler_params=pltpu.CompilerParams(vmem_limit_bytes=48 << 20),
        name="whiten",
    )(u, v, flags, jnp.asarray(even), jnp.asarray(odd), jnp.asarray(window_ones()))


WORK = jnp.float32


def solution(mesh):
    pairs, hours = mesh.shape["pairs"], mesh.shape["hours"]
    width = 1 << ((pairs.bit_length() - 1) // 2)

    def body(records, usable, pair_blocks):
        rows = records.shape[0]
        whitened = whiten(records, usable)
        marks = jnp.broadcast_to(usable.astype(jnp.bfloat16).reshape(1, rows), (16, rows))
        bj, bi, bf = exchange(pair_blocks, whitened, marks, pairs, width, hours)
        me = lax.axis_index("hours").astype(jnp.int32).reshape(1)
        return stack(me, bi, bj, bf, jnp.asarray(lag_weights()), WORK)

    return jax.shard_map(
        body,
        mesh=mesh,
        in_specs=(P("pairs", "hours", None), P("pairs", "hours"), P("pairs", None)),
        out_specs=P("pairs", "hours", None, None),
        check_vma=False,
    )
```

```python
import functools
import math

import jax
import jax.numpy as jnp
import numpy as np
from jax import lax
from jax.experimental import pallas as pl
from jax.experimental.pallas import tpu as pltpu
from jax.sharding import PartitionSpec as P

L = 3600
F = 512
W = 32
F0 = 64
LAGS = 256
EXTENT = F + 2 * W
HALF = L // 2
HE = EXTENT // 2
HF = F // 2
CORES = 2
MESH = pl.DeviceIdType.MESH


def cos_sin(phases, length, scale):
    angles = np.float32(2.0 * math.pi / length) * (phases % length).astype(np.float32)
    wide = angles.astype(np.float64)
    scale = np.float32(scale)
    return np.cos(wide).astype(np.float32) * scale, -np.sin(wide).astype(np.float32) * scale


CHUNK = 128
CHUNKS = F // CHUNK


def spectrum_tables():
    bins = F0 - W + np.arange(EXTENT)
    c, q = cos_sin(bins[:, None] * np.arange(HALF)[None, :], L, 1.0 / math.sqrt(L))
    even = np.concatenate([c[0::2], q[0::2]], axis=0)
    odd = np.concatenate([c[1::2], q[1::2]], axis=0)
    return even.astype(jnp.bfloat16), odd.astype(jnp.bfloat16)


def window_ones():
    source = np.concatenate([np.arange(0, EXTENT, 2), np.arange(1, EXTENT, 2)])
    target = np.concatenate([np.arange(0, F, 2), np.arange(1, F, 2)])
    gap = source[None, :] - target[:, None]
    return ((gap >= 0) & (gap <= 2 * W)).astype(np.float32).astype(jnp.bfloat16)


def lag_weights():
    order = np.concatenate([np.arange(0, F, 2), np.arange(1, F, 2)])
    shifts = np.arange(LAGS) - LAGS // 2
    c, s = cos_sin((F0 + order)[:, None] * shifts[None, :], L, 1.0 / math.sqrt(F))
    pieces = []
    for k in range(0, F, CHUNK):
        pieces += [c[k : k + CHUNK], s[k : k + CHUNK]]
    return np.concatenate(pieces, axis=0).astype(jnp.bfloat16)


def split_hi_lo(value):
    high = value.astype(jnp.bfloat16)
    low = (value - high.astype(jnp.float32)).astype(jnp.bfloat16)
    return jnp.concatenate([high, low], axis=1)


def whiten_kernel(
    x_ref, use_ref, even_hbm, odd_hbm, ones_hbm, out_ref, mark_ref, even, odd, ones, sem
):
    stations = x_ref.shape[1]
    loads = [
        pltpu.make_async_copy(src, dst, sem.at[k])
        for k, (src, dst) in enumerate(((even_hbm, even), (odd_hbm, odd), (ones_hbm, ones)))
    ]
    for load in loads:
        load.start()
    flags = use_ref[...].astype(jnp.float32)
    mark_ref[...] = jnp.broadcast_to(flags, mark_ref.shape).astype(jnp.bfloat16)
    early = x_ref[:HALF].astype(jnp.float32)
    late = x_ref[HALF:].astype(jnp.float32)

    def transform(load, table, signal):
        signal = split_hi_lo(signal)
        load.wait()
        both = jnp.dot(table[...], signal, preferred_element_type=jnp.float32)
        both = both[:, :stations] + both[:, stations:]
        return both[:HE], both[HE:]

    re_even, im_even = transform(loads[0], even, early + late)
    re_odd, im_odd = transform(loads[1], odd, early - late)
    power = jnp.concatenate(
        [re_even * re_even + im_even * im_even, re_odd * re_odd + im_odd * im_odd], axis=0
    )
    loads[2].wait()
    total = jnp.dot(ones[...], split_hi_lo(power), preferred_element_type=jnp.float32)
    smooth = (total[:, :stations] + total[:, stations:]) * jnp.float32(1.0 / (2 * W + 1))
    weight = flags / jnp.sqrt(smooth + 1e-05)
    w2 = W // 2
    for k in range(CHUNKS):
        at = k * CHUNK
        real, imag = (re_even, im_even) if at < HF else (re_odd, im_odd)
        inner = w2 + at % HF
        scale = weight[at : at + CHUNK]
        out_ref[k, :, :CHUNK] = (real[inner : inner + CHUNK] * scale).T.astype(jnp.bfloat16)
        out_ref[k, :, CHUNK:] = (imag[inner : inner + CHUNK] * scale).T.astype(jnp.bfloat16)


def exchange_kernel(
    pairs, width, hours, pair_ref, w_ref, f_ref, bj, bi, bf,
    *scratch,
):
    rows = w_ref.shape[1]
    part = rows // hours
    span_rows = rows // SPLIT
    units = CHUNKS * SPLIT
    g = scratch[:units]
    (
        gf, sj, si, sf, zx_send, zx_recv, j_send, j_recv, relay_send, i_send, i_recv,
        f_send, f_recv, local_sem, i_local,
    ) = scratch[units:]
    depth = pairs // width
    p = lax.axis_index("pairs")
    me = lax.axis_index("hours")
    z, x = p // width, p % width
    y, core = me // CORES, me % CORES
    partner = y * CORES + (1 - core)
    flags_unit = units

    def place(u):
        return u // SPLIT, pl.ds((u % SPLIT) * span_rows, span_rows)

    steps = (
        (z + 1 < depth, p + width),
        (z > 0, p - width),
        (x + 1 < width, p + 1),
        (x > 0, p - 1),
    )

    barrier = pltpu.get_barrier_semaphore()
    for exists, target in steps:
        @pl.when(exists)
        def _(target=target):
            pl.semaphore_signal(barrier, inc=1, device_id={"pairs": target}, device_id_type=MESH)
    for k in range(1, hours):
        pl.semaphore_signal(
            barrier, inc=1, device_id={"hours": (me + k) % hours}, device_id_type=MESH
        )
    near = sum(e.astype(jnp.int32) for e, _ in steps)
    pl.semaphore_wait(barrier, near + hours - 1)

    pending = []

    def slot(b, u):
        return gf.at[b] if u == flags_unit else g[u].at[b]

    def own(u):
        return f_ref if u == flags_unit else w_ref.at[place(u)]

    def forward(cond, b, u, way, is_own=False):
        exists, target = steps[way]
        both = exists if cond is None else jnp.logical_and(cond, exists)

        def make():
            return pltpu.make_async_remote_copy(
                src_ref=own(u) if is_own else slot(b, u),
                dst_ref=slot(b, u),
                send_sem=zx_send.at[way, b, u],
                recv_sem=zx_recv.at[b, u],
                device_id={"pairs": target},
                device_id_type=MESH,
            )

        @pl.when(both)
        def _():
            make().start()
        pending.append((both, make))

    def arrived(b, u):
        pltpu.make_async_remote_copy(
            src_ref=slot(b, u), dst_ref=slot(b, u), send_sem=zx_send.at[0, b, u],
            recv_sem=zx_recv.at[b, u], device_id={"pairs": p}, device_id_type=MESH,
        ).wait_recv()

    def send_own(u):
        for way in range(4):
            forward(None, p, u, way, is_own=True)

    keep = [
        pltpu.make_async_copy(own(u), slot(p, u), local_sem.at[u]) for u in range(units + 1)
    ]
    for copy in keep:
        copy.start()

    def gather_z(u, d):
        for way, b, cond in (
            (0, p - d * width, z - d >= 0),
            (1, p + d * width, z + d < depth),
        ):
            @pl.when(cond)
            def _(b=b):
                arrived(b, u)
            for out in (way, 2, 3):
                forward(cond, b, u, out)

    def gather_x(u):
        for d in range(1, width):
            for zz in range(depth):
                for way, b, cond in (
                    (2, zz * width + x - d, x - d >= 0),
                    (3, zz * width + x + d, x + d < width),
                ):
                    @pl.when(cond)
                    def _(b=b):
                        arrived(b, u)
                    if width > 2:
                        forward(cond, b, u, way)

    late = []
    local = []

    def remote(src, dst, send_sem, recv_sem, target):
        copy = pltpu.make_async_remote_copy(
            src_ref=src, dst_ref=dst, send_sem=send_sem, recv_sem=recv_sem,
            device_id={"hours": target}, device_id_type=MESH,
        )
        copy.start()
        late.append(copy)

    def stay(src, dst, sem):
        copy = pltpu.make_async_copy(src, dst, sem)
        copy.start()
        local.append(copy)

    def share(u):
        keep[u].wait()
        if u == flags_unit:
            sf[0] = gf[pair_ref[0, 0]]
            sf[1] = gf[pair_ref[0, 1]]
            for k in range(1, hours):
                remote(sf, bf.at[me], f_send.at[k], f_recv.at[me], (me + k) % hours)
            stay(sf, bf.at[me], local_sem.at[units + 1])
            return
        c, span = place(u)
        sj[u] = g[u][pair_ref[0, 1]]
        si[u] = g[u][pair_ref[0, 0]]
        for k in range(1, hours // CORES):
            target = ((y + k) % (hours // CORES)) * CORES + core
            remote(sj.at[u], bj.at[me, c, span], j_send.at[k, u], j_recv.at[me, u], target)
        remote(sj.at[u], bj.at[me, c, span], j_send.at[0, u], j_recv.at[me, u], partner)
        stay(sj.at[u], bj.at[me, c, span], local_sem.at[units + 2 + u])
        share_hours = hours // SPLIT
        for k in range(share_hours):
            peer = (u % SPLIT) * share_hours + k
            rows_of = si.at[u, pl.ds(k * part, part)]

            def make(peer=peer, rows_of=rows_of):
                return pltpu.make_async_remote_copy(
                    src_ref=rows_of, dst_ref=bi.at[me, c], send_sem=i_send.at[c, peer],
                    recv_sem=i_recv.at[me, c], device_id={"hours": peer}, device_id_type=MESH,
                )

            @pl.when(me != peer)
            def _(make=make):
                make().start()
            pending.append((me != peer, make))

            @pl.when(me == peer)
            def _(rows_of=rows_of):
                pltpu.make_async_copy(rows_of, bi.at[me, c], i_local.at[c]).start()

    def got(sem, ref):
        pltpu.make_async_remote_copy(
            src_ref=ref, dst_ref=ref, send_sem=sem, recv_sem=sem,
            device_id={"hours": me}, device_id_type=MESH,
        ).wait_recv()

    def relay(u):
        c, span = place(u)
        for k in range(1, hours // CORES):
            peer = ((y + k) % (hours // CORES)) * CORES + core
            piece = bj.at[peer, c, span]
            got(j_recv.at[peer, u], piece)
            remote(piece, piece, relay_send.at[k, u], j_recv.at[peer, u], partner)

    order = [flags_unit] + list(range(units))
    for t in range(len(order) + depth + 2):
        if t < len(order):
            for way in (2, 0, 1, 3):
                forward(None, p, order[t], way, is_own=True)
        for d in range(1, depth):
            if 0 <= t - d < len(order):
                gather_z(order[t - d], d)
        if 0 <= t - depth < len(order):
            gather_x(order[t - depth])
            share(order[t - depth])
        if 1 <= t - depth - 2 < len(order):
            relay(order[t - depth - 2])

    for u in range(units):
        c, span = place(u)
        for k in range(hours // CORES):
            peer = ((y + k) % (hours // CORES)) * CORES + (1 - core)
            got(j_recv.at[peer, u], bj.at[peer, c, span])
    for k in range(1, hours):
        peer = (me + k) % hours
        for c in range(CHUNKS):
            got(i_recv.at[peer, c], bi.at[peer, c])
        got(f_recv.at[peer], bf.at[peer])
    for copy in local:
        copy.wait()
    for c in range(CHUNKS):
        pltpu.make_async_copy(bi.at[me, c], bi.at[me, c], i_local.at[c]).wait()
    for cond, make in pending:
        @pl.when(cond)
        def _(make=make):
            make().wait_send()
    for copy in late:
        copy.wait_send()


SPLIT = 2


def exchange(pair_blocks, whitened, marks, pairs, width, hours):
    rows, cols = whitened.shape[1:]
    part = rows // hours
    units = CHUNKS * SPLIT
    any_space = pl.BlockSpec(memory_space=pl.ANY)
    dma = pltpu.SemaphoreType.DMA
    groups = hours // CORES
    return pl.pallas_call(
        functools.partial(exchange_kernel, pairs, width, hours),
        out_shape=(
            jax.ShapeDtypeStruct((hours, CHUNKS, rows, cols), jnp.bfloat16),
            jax.ShapeDtypeStruct((hours, CHUNKS, part, cols), jnp.bfloat16),
            jax.ShapeDtypeStruct((hours, 2) + marks.shape, jnp.bfloat16),
        ),
        in_specs=[pl.BlockSpec(memory_space=pltpu.SMEM), any_space, any_space],
        out_specs=(any_space, any_space, any_space),
        scratch_shapes=[pltpu.VMEM((pairs, rows // SPLIT, cols), jnp.bfloat16)] * units + [
            pltpu.VMEM((pairs,) + marks.shape, jnp.bfloat16),
            pltpu.VMEM((units, rows // SPLIT, cols), jnp.bfloat16),
            pltpu.VMEM((units, rows // SPLIT, cols), jnp.bfloat16),
            pltpu.VMEM((2,) + marks.shape, jnp.bfloat16),
            dma((4, pairs, units + 1)),
            dma((pairs, units + 1)),
            dma((groups, units)),
            dma((hours, units)),
            dma((groups, units)),
            dma((CHUNKS, hours)),
            dma((hours, CHUNKS)),
            dma((hours,)),
            dma((hours,)),
            dma((2 * units + 2,)),
            dma((CHUNKS,)),
        ],
        compiler_params=pltpu.CompilerParams(
            collective_id=0, has_side_effects=True, vmem_limit_bytes=32 << 20
        ),
        name="exchange",
    )(pair_blocks, whitened, marks)


GROUP = 8
SUB = 2
BLOCK = 16


def stack_kernel(
    hours, me_ref, bi_ref, bj_ref, bf_ref, g_ref, out_ref, af, heads, recip, *cross
):
    step = pl.program_id(0)
    rows = bj_ref.shape[2]
    first_rows = bi_ref.shape[2]
    f32 = jnp.float32

    @pl.when(step == 0)
    def _():
        af[...] = bi_ref[...].astype(f32)
        first = bf_ref[:, 0, 0, :]
        second = bf_ref[:, 1, 0, :]
        counts = lax.dot_general(
            second, first, (((0,), (0,)), ((), ())), preferred_element_type=f32
        )
        recip[...] = 1.0 / jnp.maximum(counts, 1.0)

    offset = me_ref[0] * first_rows + step * GROUP
    scale = pltpu.roll(recip[...], (rows - offset) % rows, 1)
    at_rows = pl.ds(pl.multiple_of(step * GROUP, GROUP), GROUP)
    for h in range(hours):
        for c in range(CHUNKS):
            ar = af[h, c, at_rows, :CHUNK]
            ai = af[h, c, at_rows, CHUNK:]
            for k, value in enumerate((ar, ar + ai, ai - ar)):
                for a in range(GROUP):
                    heads[a, c, h, k] = jnp.broadcast_to(value[a : a + 1], (8, CHUNK))

    def wide(value):
        return jnp.concatenate([value] * (BLOCK // 8), axis=0)

    for sub in range(GROUP // SUB):
        buf = cross[sub]
        for c in range(CHUNKS):
            lo = 2 * CHUNK * c
            hi = lo + CHUNK
            for r in range(0, rows, BLOCK):
                tails = []
                for h in range(hours):
                    br = bj_ref[h, c, r : r + BLOCK, :CHUNK].astype(f32)
                    bm = bj_ref[h, c, r : r + BLOCK, CHUNK:].astype(f32)
                    tails.append((br - bm, bm, br))
                for a in range(SUB):
                    sums = [None, None, None]
                    for h in range(hours):
                        for k in range(3):
                            term = wide(heads[sub * SUB + a, c, h, k]) * tails[h][k]
                            sums[k] = term if sums[k] is None else sums[k] + term
                    at = a * rows + r
                    buf[at : at + BLOCK, lo:hi] = (sums[0] + sums[1]).astype(jnp.bfloat16)
                    buf[at : at + BLOCK, hi : hi + CHUNK] = (sums[0] + sums[2]).astype(
                        jnp.bfloat16
                    )
        lagged = jnp.dot(buf[...], g_ref[...], preferred_element_type=f32)
        for a in range(SUB):
            k = sub * SUB + a
            out_ref[0, k] = lagged[a * rows : (a + 1) * rows] * scale[:, k : k + 1]


def stack(me, bi, bj, bf, weights):
    hours, _, first_rows, cols = bi.shape
    rows = bj.shape[2]
    full = lambda a: pl.BlockSpec(a.shape, lambda i, *_: (0,) * a.ndim, pipeline_mode=pl.Buffered(1))
    return pl.pallas_call(
        functools.partial(stack_kernel, hours),
        grid_spec=pltpu.PrefetchScalarGridSpec(
            num_scalar_prefetch=1,
            grid=(first_rows // GROUP,),
            in_specs=[full(bi), full(bj), full(bf), full(weights)],
            out_specs=pl.BlockSpec((1, GROUP, rows, LAGS), lambda i, *_: (0, i, 0, 0)),
            scratch_shapes=[
                pltpu.VMEM((hours, CHUNKS, first_rows, cols), jnp.float32),
                pltpu.VMEM((GROUP, CHUNKS, hours, 3, 8, CHUNK), jnp.float32),
                pltpu.VMEM((rows, rows), jnp.float32),
            ]
            + [pltpu.VMEM((SUB * rows, 2 * F), jnp.bfloat16)] * (GROUP // SUB),
        ),
        out_shape=jax.ShapeDtypeStruct((1, first_rows, rows, LAGS), jnp.float32),
        compiler_params=pltpu.CompilerParams(vmem_limit_bytes=48 << 20),
        name="stack",
    )(me, bi, bj, bf, weights)


def whiten(records, usable):
    rows = records.shape[0]
    samples = records.reshape(rows, L).T
    even, odd = spectrum_tables()
    tables = (jnp.asarray(even), jnp.asarray(odd), jnp.asarray(window_ones()))
    vmem = pl.BlockSpec(memory_space=pltpu.VMEM)
    hbm = pl.BlockSpec(memory_space=pltpu.HBM)
    return pl.pallas_call(
        whiten_kernel,
        out_shape=(
            jax.ShapeDtypeStruct((CHUNKS, rows, 2 * CHUNK), jnp.bfloat16),
            jax.ShapeDtypeStruct((16, rows), jnp.bfloat16),
        ),
        in_specs=[vmem, vmem, hbm, hbm, hbm],
        out_specs=(vmem, vmem),
        scratch_shapes=[pltpu.VMEM(t.shape, t.dtype) for t in tables]
        + [pltpu.SemaphoreType.DMA((3,))],
        compiler_params=pltpu.CompilerParams(vmem_limit_bytes=48 << 20),
        name="whiten",
    )(samples, usable.reshape(1, rows), *tables)


def solution(mesh):
    pairs, hours = mesh.shape["pairs"], mesh.shape["hours"]
    width = 1 << ((pairs.bit_length() - 1) // 2)

    def body(records, usable, pair_blocks):
        whitened, marks = whiten(records, usable)
        bj, bi, bf = exchange(pair_blocks, whitened, marks, pairs, width, hours)
        me = lax.axis_index("hours").astype(jnp.int32).reshape(1)
        return stack(me, bi, bj, bf, jnp.asarray(lag_weights()))

    return jax.shard_map(
        body,
        mesh=mesh,
        in_specs=(P("pairs", "hours", None), P("pairs", "hours"), P("pairs", None)),
        out_specs=P("pairs", "hours", None, None),
        check_vma=False,
    )
```

```python
import functools
import math

import jax
import jax.numpy as jnp
import numpy as np
from jax import lax
from jax.experimental import pallas as pl
from jax.experimental.pallas import tpu as pltpu
from jax.sharding import PartitionSpec as P

L = 3600
F = 512
W = 32
F0 = 64
LAGS = 256
EXTENT = F + 2 * W
HALF = L // 2
HE = EXTENT // 2
HF = F // 2
CORES = 2
MESH = pl.DeviceIdType.MESH


def cos_sin(phases, length, scale):
    angles = np.float32(2.0 * math.pi / length) * (phases % length).astype(np.float32)
    wide = angles.astype(np.float64)
    scale = np.float32(scale)
    return np.cos(wide).astype(np.float32) * scale, -np.sin(wide).astype(np.float32) * scale


CHUNK = 128
CHUNKS = F // CHUNK


def spectrum_tables():
    bins = F0 - W + np.arange(EXTENT)
    c, q = cos_sin(bins[:, None] * np.arange(HALF)[None, :], L, 1.0 / math.sqrt(L))
    even = np.concatenate([c[0::2], q[0::2]], axis=0)
    odd = np.concatenate([c[1::2], q[1::2]], axis=0)
    return even.astype(jnp.bfloat16), odd.astype(jnp.bfloat16)


def window_ones():
    source = np.concatenate([np.arange(0, EXTENT, 2), np.arange(1, EXTENT, 2)])
    target = np.concatenate([np.arange(0, F, 2), np.arange(1, F, 2)])
    gap = source[None, :] - target[:, None]
    return ((gap >= 0) & (gap <= 2 * W)).astype(np.float32).astype(jnp.bfloat16)


def lag_weights():
    order = np.concatenate([np.arange(0, F, 2), np.arange(1, F, 2)])
    shifts = np.arange(LAGS) - LAGS // 2
    c, s = cos_sin((F0 + order)[:, None] * shifts[None, :], L, 1.0 / math.sqrt(F))
    pieces = []
    for k in range(0, F, CHUNK):
        pieces += [c[k : k + CHUNK], s[k : k + CHUNK]]
    return np.concatenate(pieces, axis=0).astype(jnp.bfloat16)


def split_hi_lo(value):
    high = value.astype(jnp.bfloat16)
    low = (value - high.astype(jnp.float32)).astype(jnp.bfloat16)
    return jnp.concatenate([high, low], axis=1)


def whiten_kernel(
    x_ref, use_ref, even_hbm, odd_hbm, ones_hbm, out_ref, mark_ref, even, odd, ones, sem
):
    stations = x_ref.shape[1]
    loads = [
        pltpu.make_async_copy(src, dst, sem.at[k])
        for k, (src, dst) in enumerate(((even_hbm, even), (odd_hbm, odd), (ones_hbm, ones)))
    ]
    for load in loads:
        load.start()
    flags = use_ref[...].astype(jnp.float32)
    mark_ref[...] = jnp.broadcast_to(flags, mark_ref.shape).astype(jnp.bfloat16)
    early = x_ref[:HALF].astype(jnp.float32)
    late = x_ref[HALF:].astype(jnp.float32)

    def transform(load, table, signal):
        signal = split_hi_lo(signal)
        load.wait()
        both = jnp.dot(table[...], signal, preferred_element_type=jnp.float32)
        both = both[:, :stations] + both[:, stations:]
        return both[:HE], both[HE:]

    re_even, im_even = transform(loads[0], even, early + late)
    re_odd, im_odd = transform(loads[1], odd, early - late)
    power = jnp.concatenate(
        [re_even * re_even + im_even * im_even, re_odd * re_odd + im_odd * im_odd], axis=0
    )
    loads[2].wait()
    total = jnp.dot(ones[...], split_hi_lo(power), preferred_element_type=jnp.float32)
    smooth = (total[:, :stations] + total[:, stations:]) * jnp.float32(1.0 / (2 * W + 1))
    weight = flags / jnp.sqrt(smooth + 1e-05)
    w2 = W // 2
    for k in range(CHUNKS):
        at = k * CHUNK
        real, imag = (re_even, im_even) if at < HF else (re_odd, im_odd)
        inner = w2 + at % HF
        scale = weight[at : at + CHUNK]
        out_ref[k, :, :CHUNK] = (real[inner : inner + CHUNK] * scale).T.astype(jnp.bfloat16)
        out_ref[k, :, CHUNK:] = (imag[inner : inner + CHUNK] * scale).T.astype(jnp.bfloat16)


def exchange_kernel(
    pairs, width, hours, pair_ref, ask_ref, w_ref, f_ref, bj, bi, bf,
    *scratch,
):
    rows = w_ref.shape[1]
    part = rows // hours
    span_rows = rows // SPLIT
    units = CHUNKS * SPLIT
    g = scratch[:units]
    (
        gf, sj, si, sf, hand, hand_f, asks, zx_send, zx_recv, j_send, j_recv, relay_send,
        i_send, i_recv, f_send, f_recv, local_sem, i_local, a_send, a_recv, x_send, x_recv,
    ) = scratch[units:]
    depth = pairs // width
    p = lax.axis_index("pairs")
    me = lax.axis_index("hours")
    z, x = p // width, p % width
    y, core = me // CORES, me % CORES
    partner = y * CORES + (1 - core)
    flags_unit = units

    def place(u):
        return u // SPLIT, pl.ds((u % SPLIT) * span_rows, span_rows)

    def beside(k):
        return z * width + (x + k) % width

    steps = (
        (z + 1 < depth, p + width),
        (z > 0, p - width),
    )

    barrier = pltpu.get_barrier_semaphore()
    for exists, target in steps:
        @pl.when(exists)
        def _(target=target):
            pl.semaphore_signal(barrier, inc=1, device_id={"pairs": target}, device_id_type=MESH)
    for k in range(1, hours):
        pl.semaphore_signal(
            barrier, inc=1, device_id={"hours": (me + k) % hours}, device_id_type=MESH
        )
    for k in range(1, width):
        pl.semaphore_signal(
            barrier, inc=1, device_id={"pairs": beside(k)}, device_id_type=MESH
        )
    near = sum(e.astype(jnp.int32) for e, _ in steps)
    pl.semaphore_wait(barrier, near + hours - 1 + width - 1)

    pending = []

    def slot(b, u):
        return gf.at[b // width] if u == flags_unit else g[u].at[b // width]

    def own(u):
        return f_ref if u == flags_unit else w_ref.at[place(u)]

    def forward(cond, b, u, way, is_own=False):
        exists, target = steps[way]
        both = exists if cond is None else jnp.logical_and(cond, exists)

        def make():
            return pltpu.make_async_remote_copy(
                src_ref=own(u) if is_own else slot(b, u),
                dst_ref=slot(b, u),
                send_sem=zx_send.at[way, b // width, u],
                recv_sem=zx_recv.at[b // width, u],
                device_id={"pairs": target},
                device_id_type=MESH,
            )

        @pl.when(both)
        def _():
            make().start()
        pending.append((both, make))

    def arrived(b, u):
        pltpu.make_async_remote_copy(
            src_ref=slot(b, u), dst_ref=slot(b, u), send_sem=zx_send.at[0, b // width, u],
            recv_sem=zx_recv.at[b // width, u], device_id={"pairs": p}, device_id_type=MESH,
        ).wait_recv()

    def send_own(u):
        for way in range(4):
            forward(None, p, u, way, is_own=True)

    keep = [
        pltpu.make_async_copy(own(u), slot(p, u), local_sem.at[u]) for u in range(units + 1)
    ]
    for copy in keep:
        copy.start()

    def gather_z(u, d):
        for way, b, cond in (
            (0, p - d * width, z - d >= 0),
            (1, p + d * width, z + d < depth),
        ):
            @pl.when(cond)
            def _(b=b):
                arrived(b, u)
            forward(cond, b, u, way)

    def crossing(k, u):
        hand_of = hand_f.at[k - 1] if u == flags_unit else hand.at[k - 1, u]
        dst = gf if u == flags_unit else g[u]
        return pltpu.make_async_remote_copy(
            src_ref=hand_of,
            dst_ref=dst.at[pl.ds(depth + 2 * (width - k - 1), 2)],
            send_sem=x_send.at[k - 1, u],
            recv_sem=x_recv.at[width - k - 1, u],
            device_id={"pairs": beside(k)},
            device_id_type=MESH,
        )

    def offer(u):
        keep[u].wait()
        pool = gf if u == flags_unit else g[u]
        for k in range(1, width):
            for s in range(2):
                asked = asks[k - 1, s, 0:1, 0:1].astype(jnp.float32)
                picked = None
                for zz in range(depth):
                    mark = jnp.where(asked == (zz * width + x).astype(jnp.float32), 1.0, 0.0)
                    term = pool[zz].astype(jnp.float32) * mark
                    picked = term if picked is None else picked + term
                if u == flags_unit:
                    hand_f[k - 1, s] = picked.astype(jnp.bfloat16)
                else:
                    hand[k - 1, u, s] = picked.astype(jnp.bfloat16)
            crossing(k, u).start()

    def chosen(s):
        b = pair_ref[0, s]
        away = lax.rem(lax.rem(b, width) - x + width, width)
        return jnp.where(away == 0, b // width, depth + 2 * (away - 1) + s)

    late = []
    local = []

    def remote(src, dst, send_sem, recv_sem, target):
        copy = pltpu.make_async_remote_copy(
            src_ref=src, dst_ref=dst, send_sem=send_sem, recv_sem=recv_sem,
            device_id={"hours": target}, device_id_type=MESH,
        )
        copy.start()
        late.append(copy)

    def stay(src, dst, sem):
        copy = pltpu.make_async_copy(src, dst, sem)
        copy.start()
        local.append(copy)

    def share(u):
        for k in range(1, width):
            crossing(width - k, u).wait_recv()
        if u == flags_unit:
            sf[0] = gf[chosen(0)]
            sf[1] = gf[chosen(1)]
            for k in range(1, hours):
                remote(sf, bf.at[me], f_send.at[k], f_recv.at[me], (me + k) % hours)
            stay(sf, bf.at[me], local_sem.at[units + 1])
            return
        c, span = place(u)
        sj[u] = g[u][chosen(1)]
        si[u] = g[u][chosen(0)]
        for k in range(1, hours // CORES):
            target = ((y + k) % (hours // CORES)) * CORES + core
            remote(sj.at[u], bj.at[me, c, span], j_send.at[k, u], j_recv.at[me, u], target)
        remote(sj.at[u], bj.at[me, c, span], j_send.at[0, u], j_recv.at[me, u], partner)
        stay(sj.at[u], bj.at[me, c, span], local_sem.at[units + 2 + u])
        share_hours = hours // SPLIT
        for k in range(share_hours):
            peer = (u % SPLIT) * share_hours + k
            rows_of = si.at[u, pl.ds(k * part, part)]

            def make(peer=peer, rows_of=rows_of):
                return pltpu.make_async_remote_copy(
                    src_ref=rows_of, dst_ref=bi.at[me, c], send_sem=i_send.at[c, peer],
                    recv_sem=i_recv.at[me, c], device_id={"hours": peer}, device_id_type=MESH,
                )

            @pl.when(me != peer)
            def _(make=make):
                make().start()
            pending.append((me != peer, make))

            @pl.when(me == peer)
            def _(rows_of=rows_of):
                pltpu.make_async_copy(rows_of, bi.at[me, c], i_local.at[c]).start()

    def got(sem, ref):
        pltpu.make_async_remote_copy(
            src_ref=ref, dst_ref=ref, send_sem=sem, recv_sem=sem,
            device_id={"hours": me}, device_id_type=MESH,
        ).wait_recv()

    def relay(u):
        c, span = place(u)
        for k in range(1, hours // CORES):
            peer = ((y + k) % (hours // CORES)) * CORES + core
            piece = bj.at[peer, c, span]
            got(j_recv.at[peer, u], piece)
            remote(piece, piece, relay_send.at[k, u], j_recv.at[peer, u], partner)

    def asking(k):
        return pltpu.make_async_remote_copy(
            src_ref=ask_ref, dst_ref=asks.at[width - k - 1], send_sem=a_send.at[k - 1],
            recv_sem=a_recv.at[width - k - 1], device_id={"pairs": beside(k)},
            device_id_type=MESH,
        )

    order = [flags_unit] + list(range(units))
    for k in range(1, width):
        asking(k).start()
    for t in range(len(order) + depth + 3):
        if t < len(order):
            for way in range(2):
                forward(None, p, order[t], way, is_own=True)
        for d in range(1, depth):
            if 0 <= t - d < len(order):
                gather_z(order[t - d], d)
        if t == depth - 1:
            for k in range(1, width):
                asking(width - k).wait_recv()
        if 0 <= t - depth + 1 < len(order):
            offer(order[t - depth + 1])
        if 0 <= t - depth - 1 < len(order):
            share(order[t - depth - 1])
        if 1 <= t - depth - 2 < len(order):
            relay(order[t - depth - 2])

    for k in range(1, width):
        asking(k).wait_send()
        for u in range(units + 1):
            crossing(k, u).wait_send()
    for u in range(units):
        c, span = place(u)
        for k in range(hours // CORES):
            peer = ((y + k) % (hours // CORES)) * CORES + (1 - core)
            got(j_recv.at[peer, u], bj.at[peer, c, span])
    for k in range(1, hours):
        peer = (me + k) % hours
        for c in range(CHUNKS):
            got(i_recv.at[peer, c], bi.at[peer, c])
        got(f_recv.at[peer], bf.at[peer])
    for copy in local:
        copy.wait()
    for c in range(CHUNKS):
        pltpu.make_async_copy(bi.at[me, c], bi.at[me, c], i_local.at[c]).wait()
    for cond, make in pending:
        @pl.when(cond)
        def _(make=make):
            make().wait_send()
    for copy in late:
        copy.wait_send()


SPLIT = 2


def exchange(pair_blocks, asks, whitened, marks, pairs, width, hours):
    rows, cols = whitened.shape[1:]
    part = rows // hours
    units = CHUNKS * SPLIT
    any_space = pl.BlockSpec(memory_space=pl.ANY)
    dma = pltpu.SemaphoreType.DMA
    groups = hours // CORES
    depth = pairs // width
    slots = depth + 2 * (width - 1)
    return pl.pallas_call(
        functools.partial(exchange_kernel, pairs, width, hours),
        out_shape=(
            jax.ShapeDtypeStruct((hours, CHUNKS, rows, cols), jnp.bfloat16),
            jax.ShapeDtypeStruct((hours, CHUNKS, part, cols), jnp.bfloat16),
            jax.ShapeDtypeStruct((hours, 2) + marks.shape, jnp.bfloat16),
        ),
        in_specs=[pl.BlockSpec(memory_space=pltpu.SMEM), any_space, any_space, any_space],
        out_specs=(any_space, any_space, any_space),
        scratch_shapes=[pltpu.VMEM((slots, rows // SPLIT, cols), jnp.bfloat16)] * units + [
            pltpu.VMEM((slots,) + marks.shape, jnp.bfloat16),
            pltpu.VMEM((units, rows // SPLIT, cols), jnp.bfloat16),
            pltpu.VMEM((units, rows // SPLIT, cols), jnp.bfloat16),
            pltpu.VMEM((2,) + marks.shape, jnp.bfloat16),
            pltpu.VMEM((width - 1, units, 2, rows // SPLIT, cols), jnp.bfloat16),
            pltpu.VMEM((width - 1, 2) + marks.shape, jnp.bfloat16),
            pltpu.VMEM((width - 1,) + asks.shape, asks.dtype),
            dma((2, depth, units + 1)),
            dma((depth, units + 1)),
            dma((groups, units)),
            dma((hours, units)),
            dma((groups, units)),
            dma((CHUNKS, hours)),
            dma((hours, CHUNKS)),
            dma((hours,)),
            dma((hours,)),
            dma((2 * units + 2,)),
            dma((CHUNKS,)),
            dma((width - 1,)),
            dma((width - 1,)),
            dma((width - 1, units + 1)),
            dma((width - 1, units + 1)),
        ],
        compiler_params=pltpu.CompilerParams(
            collective_id=0, has_side_effects=True, vmem_limit_bytes=32 << 20
        ),
        name="exchange",
    )(pair_blocks, asks, whitened, marks)


GROUP = 8
SUB = 2
BLOCK = 16


def stack_kernel(
    hours, me_ref, bi_ref, bj_ref, bf_ref, g_ref, out_ref, af, heads, recip, *cross
):
    step = pl.program_id(0)
    rows = bj_ref.shape[2]
    first_rows = bi_ref.shape[2]
    f32 = jnp.float32

    @pl.when(step == 0)
    def _():
        af[...] = bi_ref[...].astype(f32)
        first = bf_ref[:, 0, 0, :]
        second = bf_ref[:, 1, 0, :]
        counts = lax.dot_general(
            second, first, (((0,), (0,)), ((), ())), preferred_element_type=f32
        )
        recip[...] = 1.0 / jnp.maximum(counts, 1.0)

    offset = me_ref[0] * first_rows + step * GROUP
    scale = pltpu.roll(recip[...], (rows - offset) % rows, 1)
    at_rows = pl.ds(pl.multiple_of(step * GROUP, GROUP), GROUP)
    for h in range(hours):
        for c in range(CHUNKS):
            ar = af[h, c, at_rows, :CHUNK]
            ai = af[h, c, at_rows, CHUNK:]
            for k, value in enumerate((ar, ai)):
                for a in range(GROUP):
                    heads[a, c, h, k] = jnp.broadcast_to(
                        value[a : a + 1], (BLOCK, CHUNK)
                    ).astype(jnp.bfloat16)

    for sub in range(GROUP // SUB):
        buf = cross[sub]
        for c in range(CHUNKS):
            lo = 2 * CHUNK * c
            hi = lo + CHUNK
            for r in range(0, rows, BLOCK):
                tails = []
                for h in range(hours):
                    tails.append(
                        (
                            bj_ref[h, c, r : r + BLOCK, :CHUNK],
                            bj_ref[h, c, r : r + BLOCK, CHUNK:],
                        )
                    )
                for a in range(SUB):
                    real = imag = None
                    for h in range(hours):
                        ar, ai = heads[sub * SUB + a, c, h, 0], heads[sub * SUB + a, c, h, 1]
                        br, bm = tails[h]
                        re = ar * br + ai * bm
                        im = ai * br - ar * bm
                        real = re if real is None else real + re
                        imag = im if imag is None else imag + im
                    at = a * rows + r
                    buf[at : at + BLOCK, lo:hi] = real
                    buf[at : at + BLOCK, hi : hi + CHUNK] = imag
        lagged = jnp.dot(buf[...], g_ref[...], preferred_element_type=f32)
        for a in range(SUB):
            k = sub * SUB + a
            out_ref[0, k] = lagged[a * rows : (a + 1) * rows] * scale[:, k : k + 1]


def stack(me, bi, bj, bf, weights):
    hours, _, first_rows, cols = bi.shape
    rows = bj.shape[2]
    full = lambda a: pl.BlockSpec(a.shape, lambda i, *_: (0,) * a.ndim, pipeline_mode=pl.Buffered(1))
    return pl.pallas_call(
        functools.partial(stack_kernel, hours),
        grid_spec=pltpu.PrefetchScalarGridSpec(
            num_scalar_prefetch=1,
            grid=(first_rows // GROUP,),
            in_specs=[full(bi), full(bj), full(bf), full(weights)],
            out_specs=pl.BlockSpec((1, GROUP, rows, LAGS), lambda i, *_: (0, i, 0, 0)),
            scratch_shapes=[
                pltpu.VMEM((hours, CHUNKS, first_rows, cols), jnp.float32),
                pltpu.VMEM((GROUP, CHUNKS, hours, 2, BLOCK, CHUNK), jnp.bfloat16),
                pltpu.VMEM((rows, rows), jnp.float32),
            ]
            + [pltpu.VMEM((SUB * rows, 2 * F), jnp.bfloat16)] * (GROUP // SUB),
        ),
        out_shape=jax.ShapeDtypeStruct((1, first_rows, rows, LAGS), jnp.float32),
        compiler_params=pltpu.CompilerParams(vmem_limit_bytes=48 << 20),
        name="stack",
    )(me, bi, bj, bf, weights)


def whiten(records, usable):
    rows = records.shape[0]
    samples = records.reshape(rows, L).T
    even, odd = spectrum_tables()
    tables = (jnp.asarray(even), jnp.asarray(odd), jnp.asarray(window_ones()))
    vmem = pl.BlockSpec(memory_space=pltpu.VMEM)
    hbm = pl.BlockSpec(memory_space=pltpu.HBM)
    return pl.pallas_call(
        whiten_kernel,
        out_shape=(
            jax.ShapeDtypeStruct((CHUNKS, rows, 2 * CHUNK), jnp.bfloat16),
            jax.ShapeDtypeStruct((16, rows), jnp.bfloat16),
        ),
        in_specs=[vmem, vmem, hbm, hbm, hbm],
        out_specs=(vmem, vmem),
        scratch_shapes=[pltpu.VMEM(t.shape, t.dtype) for t in tables]
        + [pltpu.SemaphoreType.DMA((3,))],
        compiler_params=pltpu.CompilerParams(vmem_limit_bytes=63 << 20),
        name="whiten",
    )(samples, usable.reshape(1, rows), *tables)


def solution(mesh):
    pairs, hours = mesh.shape["pairs"], mesh.shape["hours"]
    width = 1 << ((pairs.bit_length() - 1) // 2)

    def body(records, usable, pair_blocks):
        whitened, marks = whiten(records, usable)
        asks = jnp.broadcast_to(
            pair_blocks.reshape(2, 1, 1).astype(jnp.float32), (2, 8, 128)
        )
        bj, bi, bf = exchange(pair_blocks, asks, whitened, marks, pairs, width, hours)
        me = lax.axis_index("hours").astype(jnp.int32).reshape(1)
        return stack(me, bi, bj, bf, jnp.asarray(lag_weights()))

    return jax.shard_map(
        body,
        mesh=mesh,
        in_specs=(P("pairs", "hours", None), P("pairs", "hours"), P("pairs", None)),
        out_specs=P("pairs", "hours", None, None),
        check_vma=False,
    )
```
